32 devices in a mesh: dp: 16 (over z, y, core), mp: 2 (over x).
Axes of the slice: x: 2, y: 2, z: 4, core: 2. Of those that a mesh axis runs over, the one named last changes fastest.
Arguments:
- tokens: bfloat16 [1024, 5120], P('dp', 'mp'), may hold values from -6 to 6, as said below
- gate_first: bfloat16 [13824, 5120], P('dp', 'mp'), may hold values from -6 to 6
- up_first: bfloat16 [13824, 5120], P('dp', 'mp'), may hold values from -6 to 6
- down_first: bfloat16 [13824, 5120], P('dp', 'mp'), may hold values from -6 to 6
- gate_second: bfloat16 [13824, 5120], P('dp', 'mp'), may hold values from -6 to 6
- up_second: bfloat16 [13824, 5120], P('dp', 'mp'), may hold values from -6 to 6
- down_second: bfloat16 [13824, 5120], P('dp', 'mp'), may hold values from -6 to 6
- matching: int32 [13824], replicated, may hold values from 0 to 13823, as said below
Outputs:
- merged_gate: bfloat16 [13824, 5120], P('dp', 'mp')
- merged_up: bfloat16 [13824, 5120], P('dp', 'mp')
- merged_down: bfloat16 [13824, 5120], P('dp', 'mp')
- correlation: float32 [3456, 13824], P('mp', 'dp')
The draws below stay inside these ranges and needn't reach their ends.
Inputs may be any that keep to these rules, and one draw needn't show every extreme that they name: matching is a permutation; for any aligned block of 864 positions and any aligned block of 864 values, at most 54 of the block's entries lie in that block of values, and in every draw some pair of blocks holds exactly 54. `tokens`: each token's 5120 features have a mean square within a few hundredths of 1.
All inputs are finite; a program needn't handle non-finite values.
Results may differ from the reference program's by a relative error of at most 0.028.
Values may be sent and summed in bfloat16 or wider, within the bound.
A program may use at most 128 MiB of HBM per device.

```python
import math
import jax
import jax.numpy as jnp
from jax import lax

D = 5120
FF = 13824
CROWS = 216
TOKENS = 1024
N_DP = 16
N_MP = 2


def draw_matching(key, part):
    unit_count = FF // N_DP
    key_dest = jax.random.fold_in(key, 11)
    key_blocks = jax.random.fold_in(key, 12)
    key_source = jax.random.fold_in(key, 13)
    dest_shuffle = jax.vmap(lambda sub: jax.random.permutation(sub, unit_count))(jax.random.split(key_dest, N_DP))
    block_order = jax.random.permutation(key_blocks, N_DP)
    source_shuffle = jax.vmap(lambda sub: jax.random.permutation(sub, unit_count))(jax.random.split(key_source, N_DP))
    dest_ids = jnp.arange(N_DP, dtype=jnp.int32)[:, None]
    ranked = dest_shuffle.astype(jnp.int32) * N_DP + dest_ids
    source_block = ranked // unit_count
    source_offset = ranked % unit_count
    blocks = block_order.astype(jnp.int32)[source_block]
    offsets = source_shuffle.astype(jnp.int32)[blocks, source_offset]
    return (blocks * unit_count + offsets).reshape(-1).astype(jnp.int32)


def draw_tokens(key, part):
    key_rough = jax.random.fold_in(key, 21)
    raw = jax.random.normal(key_rough, (TOKENS, D), jnp.float32)
    raw = jnp.clip(raw, -5.0, 5.0)
    spread = jnp.sqrt(jnp.mean(raw * raw, axis=1, keepdims=True))
    return (raw / spread).astype(jnp.bfloat16)


def steps_of(rng, shape, cuts, low, top_value):
    factor_of, own = 1.0, jax.random.fold_in(rng, 6)
    for axis_at, parts in cuts:
        steps = jnp.exp(jax.random.uniform(jax.random.fold_in(own, axis_at), (parts,), jnp.float32, low / len(cuts), top_value / len(cuts)))
        factor_of = factor_of * jnp.repeat(steps, shape[axis_at] // parts).reshape([-1 if axis == axis_at else 1 for axis in range(len(shape))])
    return factor_of


def normal_values(rng, extent, scale, bound, shards=(), kind=jnp.bfloat16):
    drawn = jax.random.normal(rng, extent, jnp.float32) * scale
    if len(shards) > 0:
        drawn = steps_of(rng, extent, shards, -0.22, 0.18) * drawn
    return jnp.clip(drawn, min=-bound, max=bound).astype(kind)


def setup_inputs(seed: int = 0) -> dict:
    splits = jax.random.split(jax.random.key(seed), 9)
    return {
        "tokens": draw_tokens(jax.random.fold_in(splits[8], 71), 0),
        "gate_first": normal_values(splits[1], (FF, D), 1.0, 6.0, ((0, 16), (1, 2))),
        "up_first": normal_values(splits[2], (FF, D), 1.0, 6.0, ((0, 16), (1, 2))),
        "down_first": normal_values(splits[3], (FF, D), 1.0, 6.0, ((0, 16), (1, 2))),
        "gate_second": normal_values(splits[4], (FF, D), 1.0, 6.0, ((0, 16), (1, 2))),
        "up_second": normal_values(splits[5], (FF, D), 1.0, 6.0, ((0, 16), (1, 2))),
        "down_second": normal_values(splits[6], (FF, D), 1.0, 6.0, ((0, 16), (1, 2))),
        "matching": draw_matching(jax.random.fold_in(splits[8], 71), 0),
    }


def projected(inputs, weight):
    feature_cols = D // N_MP
    factor = 1.0 / math.sqrt(D)
    summed = jnp.zeros((TOKENS, FF), jnp.float32)
    for piece in range(N_MP):
        inner = inputs[:, piece * feature_cols:(piece + 1) * feature_cols]
        outer = weight[:, piece * feature_cols:(piece + 1) * feature_cols]
        term = lax.dot_general(inner, outer, (((1,), (1,)), ((), ())), preferred_element_type=jnp.float32)
        term = (term * factor).astype(jnp.bfloat16)
        term = lax.optimization_barrier(term)
        summed = summed + term.astype(jnp.float32)
    return summed

def averaged(first, second, matching):
    moved = jnp.take(second, matching, axis=0)
    return ((first.astype(jnp.float32) + moved.astype(jnp.float32)) * 0.5).astype(jnp.bfloat16)

def reference(tokens, gate_first, up_first, down_first, gate_second, up_second, down_second, matching):
    hidden_first = (jax.nn.silu(projected(tokens, gate_first)) * projected(tokens, up_first)).astype(jnp.bfloat16)
    hidden_second = (jax.nn.silu(projected(tokens, gate_second)) * projected(tokens, up_second)).astype(jnp.bfloat16)
    window = hidden_first.reshape(TOKENS, N_DP, FF // N_DP)[:, :, :CROWS].reshape(TOKENS, CROWS * N_DP)
    chosen = jnp.take(hidden_second, matching, axis=1)
    correlation = lax.dot_general(window, chosen, (((0,), (0,)), ((), ())), preferred_element_type=jnp.float32)
    correlation = correlation / math.sqrt(TOKENS)
    return (averaged(gate_first, gate_second, matching), averaged(up_first, up_second, matching), averaged(down_first, down_second, matching), correlation)
```

```python
import math

import jax
import jax.numpy as jnp
from jax import lax
from jax.sharding import PartitionSpec as P

D = 5120
CROWS = 216


def matmul_t(a, b):
    return lax.dot_general(a, b, (((1,), (1,)), ((), ())), preferred_element_type=jnp.float32)


def pick(onehot, rows):
    return jnp.dot(onehot, rows, preferred_element_type=jnp.float32).astype(jnp.bfloat16)


def local(tokens, gate_first, up_first, down_first, gate_second, up_second, down_second, matching):
    data_size = lax.axis_size("dp")
    model_size = lax.axis_size("mp")
    position = lax.axis_index("dp")
    unit_count = gate_first.shape[0]
    feature_cols = gate_first.shape[1]
    capacity = -(-unit_count // data_size)
    slots = data_size * capacity
    factor = 1.0 / math.sqrt(D)

    everyone = lax.all_gather(tokens, "dp", axis=0, tiled=True)
    token_count = everyone.shape[0]

    routing = matching.reshape(data_size, unit_count)
    owners = lax.div(routing, unit_count)
    offsets = routing - owners * unit_count
    owned = owners == position
    unit_ids = jnp.arange(unit_count, dtype=jnp.int32)
    before = (unit_ids[:, None] < unit_ids[None, :]).astype(jnp.bfloat16)
    ranking = jnp.dot(owned.astype(jnp.bfloat16), before, preferred_element_type=jnp.float32)
    ranking = ranking.astype(jnp.int32)
    slot_ids = jnp.arange(capacity, dtype=jnp.int32)
    matches = owned[:, None, :] & (ranking[:, None, :] == slot_ids[None, :, None])
    send_index = jnp.sum(jnp.where(matches, offsets[:, None, :], 0), axis=2).reshape(-1)
    chooser = (send_index[:, None] == unit_ids[None, :]).astype(jnp.bfloat16)

    sources = lax.dynamic_slice_in_dim(matching, position * unit_count, unit_count)
    source_block = lax.div(sources, unit_count)
    earlier = (source_block[None, :] == source_block[:, None]) & (
        unit_ids[None, :] < unit_ids[:, None]
    )
    landing = source_block * capacity + jnp.sum(earlier.astype(jnp.int32), axis=1)
    placer = (landing[:, None] == jnp.arange(slots, dtype=jnp.int32)[None, :]).astype(jnp.bfloat16)

    def exchange(rows):
        return lax.all_to_all(
            rows.reshape(data_size, capacity, -1), "dp", split_axis=0, concat_axis=0, tiled=True
        ).reshape(slots, -1)

    def averaged(first, moved):
        return ((first.astype(jnp.float32) + moved.astype(jnp.float32)) * 0.5).astype(jnp.bfloat16)

    def hidden(rows):
        count = rows.shape[0] // 2
        term = (matmul_t(everyone, rows) * factor).astype(jnp.bfloat16)
        parts = lax.all_to_all(
            term.reshape(model_size, -1, 2 * count), "mp", split_axis=0, concat_axis=0, tiled=True
        )
        pre = jnp.sum(parts.astype(jnp.float32), axis=0)
        return (jax.nn.silu(pre[:, :count]) * pre[:, count:]).astype(jnp.bfloat16)

    gate_out = pick(chooser, gate_second)
    up_out = pick(chooser, up_second)
    gate_in = exchange(gate_out)
    up_in = exchange(up_out)
    down_out = pick(chooser, down_second)

    window = hidden(jnp.concatenate([gate_first[:CROWS], up_first[:CROWS]], axis=0))
    window = lax.all_gather(window, "dp", axis=1, tiled=True)
    window = lax.all_to_all(window, "mp", split_axis=1, concat_axis=0, tiled=True)

    down_out, up_in, gate_in = lax.optimization_barrier((down_out, up_in, gate_in))
    down_in = exchange(down_out)
    gate_moved = pick(placer, gate_in)
    up_moved = pick(placer, up_in)
    chosen = hidden(jnp.concatenate([gate_moved, up_moved], axis=0))
    chosen = lax.all_gather(chosen, "mp", axis=0, tiled=True)
    merged_gate = averaged(gate_first, gate_moved)
    merged_up = averaged(up_first, up_moved)
    merged_down = averaged(down_first, pick(placer, down_in))
    correlation = lax.dot_general(
        window, chosen, (((0,), (0,)), ((), ())), preferred_element_type=jnp.float32
    ) / math.sqrt(token_count)
    return (merged_gate, merged_up, merged_down, correlation)


def solution(mesh):
    in_specs = (P("dp", "mp"),) * 7 + (P(),)
    out_specs = (P("dp", "mp"), P("dp", "mp"), P("dp", "mp"), P("mp", "dp"))
    return jax.shard_map(local, mesh=mesh, in_specs=in_specs, out_specs=out_specs, check_vma=False)
```

```python
import math

import jax
import jax.numpy as jnp
from jax import lax
from jax.sharding import PartitionSpec as P

D = 5120
CROWS = 216


def matmul_t(a, b):
    return lax.dot_general(a, b, (((1,), (1,)), ((), ())), preferred_element_type=jnp.float32)


def pick(onehot, rows):
    return jnp.dot(onehot, rows, preferred_element_type=jnp.float32).astype(jnp.bfloat16)


def local(tokens, gate_first, up_first, down_first, gate_second, up_second, down_second, matching):
    data_size = lax.axis_size("dp")
    model_size = lax.axis_size("mp")
    position = lax.axis_index("dp")
    model_position = lax.axis_index("mp")
    unit_count = gate_first.shape[0]
    capacity = -(-unit_count // data_size)
    capacity = -(-capacity // 8) * 8
    slots = data_size * capacity
    factor = 1.0 / math.sqrt(D)

    parities = [list(range(parity, data_size, 2)) for parity in range(2)]
    swap = [(i, i ^ 1) for i in range(data_size)]
    even = position % 2 == 0

    def gather(block):
        return lax.all_gather(block, "dp", axis=0, axis_index_groups=parities)

    def both(mine, axis):
        other = lax.ppermute(mine, "dp", swap)
        halves = [jnp.where(even, mine, other), jnp.where(even, other, mine)]
        return jnp.stack(halves, axis=axis)

    routing = matching.reshape(data_size, unit_count)
    owners = lax.div(routing, unit_count)
    offsets = routing - owners * unit_count
    owned = owners == position
    unit_ids = jnp.arange(unit_count, dtype=jnp.int32)
    before = (unit_ids[:, None] < unit_ids[None, :]).astype(jnp.bfloat16)
    ranking = jnp.dot(owned.astype(jnp.bfloat16), before, preferred_element_type=jnp.float32)
    ranking = ranking.astype(jnp.int32)
    slot_ids = jnp.arange(capacity, dtype=jnp.int32)
    matches = owned[:, None, :] & (ranking[:, None, :] == slot_ids[None, :, None])
    send_index = jnp.sum(jnp.where(matches, offsets[:, None, :], 0), axis=2).reshape(-1)
    chooser = (send_index[:, None] == unit_ids[None, :]).astype(jnp.bfloat16)

    sources = lax.dynamic_slice_in_dim(matching, position * unit_count, unit_count)
    source_block = lax.div(sources, unit_count)
    earlier = (source_block[None, :] == source_block[:, None]) & (
        unit_ids[None, :] < unit_ids[:, None]
    )
    landing = source_block * capacity + jnp.sum(earlier.astype(jnp.int32), axis=1)
    placer = (landing[:, None] == jnp.arange(slots, dtype=jnp.int32)[None, :]).astype(jnp.bfloat16)

    def exchange(rows):
        return lax.all_to_all(
            rows.reshape(data_size, capacity, -1), "dp", split_axis=0, concat_axis=0, tiled=True
        ).reshape(slots, -1)

    def averaged(first, moved):
        return ((first.astype(jnp.float32) + moved.astype(jnp.float32)) * 0.5).astype(jnp.bfloat16)

    def shifted(value, by):
        return lax.ppermute(value, "mp", [(i, (i + by) % model_size) for i in range(model_size)])

    def shares(value, axis):
        size = value.shape[axis] // model_size
        out = []
        for by in range(model_size):
            target = (model_position + by) % model_size
            part = lax.dynamic_slice_in_dim(value, target * size, size, axis)
            out.append(part if by == 0 else shifted(part, by))
        return out

    def projected(rows):
        term = (matmul_t(rows, everyone) * factor).astype(jnp.bfloat16)
        return sum(part.astype(jnp.float32) for part in shares(term, 1))

    def hidden(gate, up):
        return (jax.nn.silu(gate) * up).astype(jnp.bfloat16)

    gate_out = pick(chooser, gate_second)
    up_out = pick(chooser, up_second)
    down_out = pick(chooser, down_second)
    mine, gate_out = lax.optimization_barrier((gather(tokens), gate_out))
    gate_in = exchange(gate_out)

    everyone = both(mine, 0).reshape(-1, tokens.shape[1])
    token_count = everyone.shape[0]
    window = hidden(projected(gate_first[:CROWS]), projected(up_first[:CROWS]))
    up_out, gate_in, window = lax.optimization_barrier((up_out, gate_in, window))
    up_in = exchange(up_out)

    window = shares(both(gather(window), 1).reshape(data_size * CROWS, -1), 0)
    gate_moved = pick(placer, gate_in)
    gate_pre = projected(gate_moved)
    down_out, up_in, gate_pre = lax.optimization_barrier((down_out, up_in, gate_pre))
    down_in = exchange(down_out)

    up_in, window = lax.optimization_barrier((up_in, window))
    up_moved = pick(placer, up_in)
    chosen = hidden(gate_pre, projected(up_moved))
    correlation = matmul_t(window[0], chosen)
    for by in range(1, model_size):
        correlation = correlation + matmul_t(window[by], shifted(chosen, by))
    correlation = correlation / math.sqrt(token_count)
    merged_gate = averaged(gate_first, gate_moved)
    merged_up = averaged(up_first, up_moved)
    merged_down = averaged(down_first, pick(placer, down_in))
    return (merged_gate, merged_up, merged_down, correlation)


def solution(mesh):
    in_specs = (P("dp", "mp"),) * 7 + (P(),)
    out_specs = (P("dp", "mp"), P("dp", "mp"), P("dp", "mp"), P("mp", "dp"))
    return jax.shard_map(local, mesh=mesh, in_specs=in_specs, out_specs=out_specs, check_vma=False)
```

```python
import math

import jax
import jax.numpy as jnp
from jax import lax
from jax.sharding import PartitionSpec as P


D = 5120
CROWS = 216


def matmul_t(a, b):
    return lax.dot_general(a, b, (((1,), (1,)), ((), ())), preferred_element_type=jnp.float32)


def pick(onehot, rows):
    return jnp.dot(onehot, rows, preferred_element_type=jnp.float32).astype(jnp.bfloat16)


def local(tokens, gate_first, up_first, down_first, gate_second, up_second, down_second, matching):
    data_size = lax.axis_size("dp")
    model_size = lax.axis_size("mp")
    position = lax.axis_index("dp")
    model_position = lax.axis_index("mp")
    unit_count = gate_first.shape[0]
    capacity = -(-unit_count // data_size)
    capacity = -(-capacity // 8) * 8
    slots = data_size * capacity
    factor = 1.0 / math.sqrt(D)

    parities = [list(range(parity, data_size, 2)) for parity in range(2)]
    swap = [(i, i ^ 1) for i in range(data_size)]
    even = position % 2 == 0

    def gather(block):
        return lax.all_gather(block, "dp", axis=0, axis_index_groups=parities)

    def both(mine, axis):
        other = lax.ppermute(mine, "dp", swap)
        halves = [jnp.where(even, mine, other), jnp.where(even, other, mine)]
        return jnp.stack(halves, axis=axis)

    routing = matching.reshape(data_size, unit_count)
    owners = lax.div(routing, unit_count)
    offsets = routing - owners * unit_count
    owned = owners == position
    unit_ids = jnp.arange(unit_count, dtype=jnp.int32)
    before = (unit_ids[:, None] < unit_ids[None, :]).astype(jnp.bfloat16)
    ranking = jnp.dot(owned.astype(jnp.bfloat16), before, preferred_element_type=jnp.float32)
    ranking = ranking.astype(jnp.int32)
    slot_ids = jnp.arange(capacity, dtype=jnp.int32)
    matches = owned[:, None, :] & (ranking[:, None, :] == slot_ids[None, :, None])
    send_index = jnp.sum(jnp.where(matches, offsets[:, None, :], 0), axis=2).reshape(-1)
    chooser = (send_index[:, None] == unit_ids[None, :]).astype(jnp.bfloat16)

    sources = lax.dynamic_slice_in_dim(matching, position * unit_count, unit_count)
    source_block = lax.div(sources, unit_count)
    earlier = (source_block[None, :] == source_block[:, None]) & (
        unit_ids[None, :] < unit_ids[:, None]
    )
    landing = source_block * capacity + jnp.sum(earlier.astype(jnp.int32), axis=1)
    placer = (landing[:, None] == jnp.arange(slots, dtype=jnp.int32)[None, :]).astype(jnp.bfloat16)

    def exchange(rows):
        return lax.all_to_all(
            rows.reshape(data_size, capacity, -1), "dp", split_axis=0, concat_axis=0, tiled=True
        ).reshape(slots, -1)

    def averaged(first, moved):
        return ((first.astype(jnp.float32) + moved.astype(jnp.float32)) * 0.5).astype(jnp.bfloat16)

    def shifted(value, by):
        return lax.ppermute(value, "mp", [(i, (i + by) % model_size) for i in range(model_size)])

    def shares(value, axis):
        size = value.shape[axis] // model_size
        out = []
        for by in range(model_size):
            target = (model_position + by) % model_size
            part = lax.dynamic_slice_in_dim(value, target * size, size, axis)
            out.append(part if by == 0 else shifted(part, by))
        return out

    def projected(rows):
        term = (matmul_t(rows, everyone) * factor).astype(jnp.bfloat16)
        return sum(part.astype(jnp.float32) for part in shares(term, 1))

    def hidden(gate, up):
        return (jax.nn.silu(gate) * up).astype(jnp.bfloat16)

    gate_out = pick(chooser, gate_second)
    up_out = pick(chooser, up_second)
    down_out = pick(chooser, down_second)
    mine = gather(tokens)
    gate_in = exchange(gate_out)

    everyone = both(mine, 0).reshape(-1, tokens.shape[1])
    token_count = everyone.shape[0]
    window = hidden(projected(gate_first[:CROWS]), projected(up_first[:CROWS]))
    up_out, gate_in, window = lax.optimization_barrier((up_out, gate_in, window))
    up_in = exchange(up_out)

    window = gather(window)
    gate_moved = pick(placer, gate_in)
    gate_pre = projected(gate_moved)
    down_out, up_in, gate_pre, window = lax.optimization_barrier(
        (down_out, up_in, gate_pre, window)
    )
    down_in = exchange(down_out)

    window = shares(both(window, 1).reshape(data_size * CROWS, -1), 0)
    up_moved = pick(placer, up_in)
    chosen = hidden(gate_pre, projected(up_moved))
    correlation = matmul_t(window[0], chosen)
    for by in range(1, model_size):
        correlation = correlation + matmul_t(window[by], shifted(chosen, by))
    correlation = correlation / math.sqrt(token_count)
    merged_gate = averaged(gate_first, gate_moved)
    merged_up = averaged(up_first, up_moved)
    merged_down = averaged(down_first, pick(placer, down_in))
    return (merged_gate, merged_up, merged_down, correlation)


def solution(mesh):
    in_specs = (P("dp", "mp"),) * 7 + (P(),)
    out_specs = (P("dp", "mp"), P("dp", "mp"), P("dp", "mp"), P("mp", "dp"))
    return jax.shard_map(local, mesh=mesh, in_specs=in_specs, out_specs=out_specs, check_vma=False)
```

```python
import math

import jax
import jax.numpy as jnp
from jax import lax
from jax.sharding import PartitionSpec as P

D = 5120
CROWS = 216


def matmul_t(a, b):
    return lax.dot_general(a, b, (((1,), (1,)), ((), ())), preferred_element_type=jnp.float32)


def pick(onehot, rows):
    return jnp.dot(onehot, rows, preferred_element_type=jnp.float32).astype(jnp.bfloat16)


def local(tokens, gate_first, up_first, down_first, gate_second, up_second, down_second, matching):
    data_size = lax.axis_size("dp")
    model_size = lax.axis_size("mp")
    position = lax.axis_index("dp")
    model_position = lax.axis_index("mp")
    unit_count = gate_first.shape[0]
    capacity = -(-unit_count // data_size)
    capacity = -(-capacity // 8) * 8
    slots = data_size * capacity
    factor = 1.0 / math.sqrt(D)

    parities = [list(range(parity, data_size, 2)) for parity in range(2)]
    lanes = [list(range(lane, data_size, 4)) for lane in range(4)]
    pairs = [[i, i + 2] for i in range(data_size) if i % 4 < 2]
    swap = [(i, i ^ 1) for i in range(data_size)]
    even = position % 2 == 0

    def both(mine, axis):
        other = lax.ppermute(mine, "dp", swap)
        halves = [jnp.where(even, mine, other), jnp.where(even, other, mine)]
        return jnp.stack(halves, axis=axis)

    routing = matching.reshape(data_size, unit_count)
    owners = lax.div(routing, unit_count)
    offsets = routing - owners * unit_count
    owned = owners == position
    unit_ids = jnp.arange(unit_count, dtype=jnp.int32)
    before = (unit_ids[:, None] < unit_ids[None, :]).astype(jnp.bfloat16)
    ranking = jnp.dot(owned.astype(jnp.bfloat16), before, preferred_element_type=jnp.float32)
    ranking = ranking.astype(jnp.int32)
    slot_ids = jnp.arange(capacity, dtype=jnp.int32)
    matches = owned[:, None, :] & (ranking[:, None, :] == slot_ids[None, :, None])
    send_index = jnp.sum(jnp.where(matches, offsets[:, None, :], 0), axis=2).reshape(-1)
    chooser = (send_index[:, None] == unit_ids[None, :]).astype(jnp.bfloat16)

    sources = lax.dynamic_slice_in_dim(matching, position * unit_count, unit_count)
    source_block = lax.div(sources, unit_count)
    earlier = (source_block[None, :] == source_block[:, None]) & (
        unit_ids[None, :] < unit_ids[:, None]
    )
    landing = source_block * capacity + jnp.sum(earlier.astype(jnp.int32), axis=1)
    placer = (landing[:, None] == jnp.arange(slots, dtype=jnp.int32)[None, :]).astype(jnp.bfloat16)

    def exchange(rows):
        return lax.all_to_all(
            rows.reshape(data_size, capacity, -1), "dp", split_axis=0, concat_axis=0, tiled=True
        ).reshape(slots, -1)

    def averaged(first, moved):
        return ((first.astype(jnp.float32) + moved.astype(jnp.float32)) * 0.5).astype(jnp.bfloat16)

    def shifted(value, by):
        return lax.ppermute(value, "mp", [(i, (i + by) % model_size) for i in range(model_size)])

    def shares(value, axis):
        size = value.shape[axis] // model_size
        out = []
        for by in range(model_size):
            target = (model_position + by) % model_size
            part = lax.dynamic_slice_in_dim(value, target * size, size, axis)
            out.append(part if by == 0 else shifted(part, by))
        return out

    def projected(rows):
        term = (matmul_t(rows, everyone) * factor).astype(jnp.bfloat16)
        return sum(part.astype(jnp.float32) for part in shares(term, 1))

    def hidden(gate, up):
        return (jax.nn.silu(gate) * up).astype(jnp.bfloat16)

    gate_out = pick(chooser, gate_second)
    up_out = pick(chooser, up_second)
    down_out = pick(chooser, down_second)
    mine = lax.all_gather(tokens, "dp", axis=0, axis_index_groups=lanes)
    mine, gate_out = lax.optimization_barrier((mine, gate_out))
    gate_in = exchange(gate_out)
    mine = lax.all_gather(mine, "dp", axis=0, axis_index_groups=pairs)

    everyone = both(mine, 0).reshape(-1, tokens.shape[1])
    token_count = everyone.shape[0]
    window = hidden(projected(gate_first[:CROWS]), projected(up_first[:CROWS]))
    up_out, gate_in, window = lax.optimization_barrier((up_out, gate_in, window))
    up_in = exchange(up_out)

    window = lax.all_gather(window, "dp", axis=0, axis_index_groups=parities)
    gate_moved = pick(placer, gate_in)
    gate_pre = projected(gate_moved)
    gate_pre, window = lax.optimization_barrier((gate_pre, window))
    window = both(window, 1)
    down_out, up_in, gate_pre, window = lax.optimization_barrier(
        (down_out, up_in, gate_pre, window)
    )
    down_in = exchange(down_out)

    window = shares(window.reshape(data_size * CROWS, -1), 0)
    up_moved = pick(placer, up_in)
    chosen = hidden(gate_pre, projected(up_moved))
    correlation = matmul_t(window[0], chosen)
    for by in range(1, model_size):
        correlation = correlation + matmul_t(window[by], shifted(chosen, by))
    correlation = correlation / math.sqrt(token_count)
    merged_gate = averaged(gate_first, gate_moved)
    merged_up = averaged(up_first, up_moved)
    merged_down = averaged(down_first, pick(placer, down_in))
    return (merged_gate, merged_up, merged_down, correlation)


def solution(mesh):
    in_specs = (P("dp", "mp"),) * 7 + (P(),)
    out_specs = (P("dp", "mp"), P("dp", "mp"), P("dp", "mp"), P("mp", "dp"))
    return jax.shard_map(local, mesh=mesh, in_specs=in_specs, out_specs=out_specs, check_vma=False)
```
